32 devices in a mesh: don: 4 (over x, core), acc: 8 (over z, y).
Axes of the slice: x: 2, y: 2, z: 4, core: 2. Of those that a mesh axis runs over, the one named last changes fastest.
Arguments:
- donor_emb: bfloat16 [65536, 768], P(('don', 'acc')), may hold values from -12 to 12
- acceptor_emb: bfloat16 [65536, 768], P(('don', 'acc')), may hold values from -6 to 6
- donor_pos: int32 [768], P(('don', 'acc')), may hold values from 0 to 2047
- acceptor_pos: int32 [768], P(('don', 'acc')), may hold values from 0 to 2047
- donor_count: int32 [32], P('don'), may hold values from 1 to 24, as said below
- acceptor_count: int32 [32], replicated, may hold values from 1 to 24, as said below
- target: int32 [64, 768], P(None, 'don'), may hold values from 0 to 767, as said below
- junction_mask: int32 [64, 768], P(None, 'don'), may hold values 0 or 1
- weights: bfloat16 [64, 768, 768], P('acc'), may hold values from -1 to 2
Outputs:
- loss: float32 [], replicated
- grad_weight: float32 [768, 64, 768], P('don', 'acc')
The draws below stay inside these ranges and needn't reach their ends.
Inputs may be any that keep to these rules, and one draw needn't show every extreme that they name: `donor_count`: the live donor slots of all shards number exactly 400; some shard has all 24 live. `acceptor_count`: the live acceptor slots of all shards number exactly 400; some shard has all 24 live. `target`: each entry names a live acceptor slot.
All inputs are finite; a program needn't handle non-finite values. No bound on the sum of `junction_mask` on one device may be relied on, other than what follows from the above.
Results may differ from the reference program's by a relative error of at most 0.0031.
Values may be sent and summed in bfloat16 or wider, within the bound.
A program may use at most 128 MiB of HBM per device.

```python
import jax
import jax.numpy as jnp
from jax import lax

D = 768
TIS = 64
CAP = 24
POS_DEV = 2048
SHARDS = 32
SEQ = 65536
DONORS = 768


def site_counts(key):
    bias_key, noise_key, chosen_key = jax.random.split(key, 3)
    extra = CAP - 1
    slots = SHARDS * extra
    needed = SHARDS * (CAP + 1) // 2 - SHARDS
    bias = jax.random.randint(bias_key, (SHARDS,), 0, 8)
    chosen = jax.random.randint(chosen_key, (), 0, SHARDS)
    bias = jnp.where(jnp.arange(SHARDS) == chosen, 12, bias)
    noise = jax.random.randint(noise_key, (SHARDS, extra), 0, 65536)
    score = noise + bias[:, None] * 16384
    order = jnp.arange(slots, dtype=jnp.int32).reshape(SHARDS, extra)
    keyed = (score * slots + order).reshape(-1).astype(jnp.int32)
    threshold = jnp.sort(keyed)[slots - needed]
    taken = (keyed >= threshold).astype(jnp.int32).reshape(SHARDS, extra)
    return (1 + jnp.sum(taken, axis=1)).astype(jnp.int32)


def draw_donor_count(key, part):
    return site_counts(jax.random.fold_in(key, 3))


def draw_acceptor_count(key, part):
    return site_counts(jax.random.fold_in(key, 5))


def draw_target(key, part):
    counts = site_counts(jax.random.fold_in(key, 5))
    shard_key, slot_key = jax.random.split(jax.random.fold_in(key, 11))
    shard = jax.random.randint(shard_key, (TIS, DONORS), 0, SHARDS)
    within = jax.random.randint(slot_key, (TIS, DONORS), 0, counts[shard])
    return (shard * CAP + within).astype(jnp.int32)


def draw_donor_emb(key, part):
    noise_key = jax.random.fold_in(jax.random.fold_in(key, 21), 0)
    values = jax.random.truncated_normal(noise_key, -6.0, 6.0, (SEQ, D), jnp.float32)
    return values.astype(jnp.bfloat16)


def draw_acceptor_emb(key, part):
    noise_key = jax.random.fold_in(key, 23)
    values = jax.random.truncated_normal(noise_key, -6.0, 6.0, (SEQ, D), jnp.float32)
    return values.astype(jnp.bfloat16)


def draw_weights(key, part):
    values = jax.random.truncated_normal(jax.random.fold_in(key, 31), -4.0, 4.0, (TIS, D, D), jnp.float32) * D ** (-0.5)
    return values.astype(jnp.bfloat16)


def touch_ends(drawn, stream_key, low, high):
    extent = drawn.shape
    spot = [jax.random.randint(jax.random.fold_in(stream_key, axis), (), 0, extent[axis]) for axis in range(len(extent))]
    drawn = drawn.at[tuple(spot)].set(low)
    longest = extent.index(max(extent))
    spot[longest] = (spot[longest] + 1) % extent[longest]
    return drawn.at[tuple(spot)].set(high)


def setup_inputs(seed: int = 0) -> dict:
    key_list = jax.random.split(jax.random.key(seed), 10)
    return {
        "donor_emb": draw_donor_emb(jax.random.fold_in(key_list[9], 71), 0),
        "acceptor_emb": draw_acceptor_emb(jax.random.fold_in(key_list[9], 71), 0),
        "donor_pos": touch_ends(jax.random.randint(key_list[2], (DONORS,), 0, POS_DEV), jax.random.fold_in(key_list[2], 1), 0, POS_DEV - 1).astype(jnp.int32),
        "acceptor_pos": touch_ends(jax.random.randint(key_list[3], (DONORS,), 0, POS_DEV), jax.random.fold_in(key_list[3], 1), 0, POS_DEV - 1).astype(jnp.int32),
        "donor_count": draw_donor_count(jax.random.fold_in(key_list[9], 71), 0),
        "acceptor_count": draw_acceptor_count(jax.random.fold_in(key_list[9], 71), 0),
        "target": draw_target(jax.random.fold_in(key_list[9], 71), 0),
        "junction_mask": touch_ends((jax.random.randint(key_list[7], (TIS, DONORS), 0, 2) < 1).astype(jnp.int32), jax.random.fold_in(key_list[7], 1), 0, 1),
        "weights": draw_weights(jax.random.fold_in(key_list[9], 71), 0),
    }


def site_rows(emb, positions):
    slot = jnp.arange(positions.shape[0], dtype=jnp.int32)
    rows = ((slot // CAP) * POS_DEV + positions).astype(jnp.int32)
    return jnp.take(emb, rows, axis=0)


def live_slots(counts):
    slot = jnp.arange(DONORS, dtype=jnp.int32)
    return (slot % CAP) < jnp.repeat(counts, CAP)


def reference(donor_emb, acceptor_emb, donor_pos, acceptor_pos, donor_count, acceptor_count, target, junction_mask, weights):
    donors = site_rows(donor_emb, donor_pos)
    acceptors = site_rows(acceptor_emb, acceptor_pos)
    live_d = live_slots(donor_count)
    live_a = live_slots(acceptor_count)
    scale = D ** -0.5
    columns = jnp.arange(DONORS, dtype=jnp.int32)

    def tissue(inputs):
        matrix, target_row, mask_row = inputs
        projected = jnp.dot(donors, matrix, preferred_element_type=jnp.float32).astype(jnp.bfloat16)
        scores = jnp.dot(projected, acceptors.T, preferred_element_type=jnp.float32) * scale
        scores = jnp.where(live_a[None, :], scores, -1e30)
        highest = jnp.max(scores, axis=1, keepdims=True)
        summed_exp = jnp.sum(jnp.where(live_a[None, :], jnp.exp(scores - highest), 0.0), axis=1, keepdims=True)
        log_total = highest + jnp.log(summed_exp)
        is_target = columns[None, :] == target_row[:, None]
        picked = jnp.sum(jnp.where(is_target, scores, 0.0), axis=1)
        weight = jnp.where(live_d, mask_row, 0).astype(jnp.float32)
        summed = jnp.sum(weight * (log_total[:, 0] - picked))
        counted = jnp.sum(weight)
        probs = jnp.where(live_a[None, :], jnp.exp(scores - log_total), 0.0)
        dscore = (weight[:, None] * (probs - is_target.astype(jnp.float32))).astype(jnp.bfloat16)
        dproj = (jnp.dot(dscore, acceptors, preferred_element_type=jnp.float32) * scale).astype(jnp.bfloat16)
        gradient = jnp.dot(donors.T, dproj, preferred_element_type=jnp.float32)
        return summed, counted, gradient

    summed, counted, gradient = lax.map(tissue, (weights, target, junction_mask))
    loss = jnp.sum(summed) / jnp.maximum(jnp.sum(counted), 1.0)
    return loss, jnp.transpose(gradient, (1, 0, 2))
```

```python
import functools

import jax
import jax.numpy as jnp
from jax import lax
from jax.experimental import pallas as pl
from jax.experimental.pallas import tpu as pltpu
from jax.sharding import PartitionSpec as P

BF16 = jnp.bfloat16
F32 = jnp.float32


def round_up(n, m):
    return (n + m - 1) // m * m


def row_chunk(n, limit=416):
    best = 16
    for r in range(16, limit + 1, 16):
        if n % r == 0:
            best = r
    return best


def ranks(counts, slots, width):
    shards = counts.shape[0]
    col = lax.broadcasted_iota(jnp.int32, (8, width), 1)

    def step(k, carry):
        first, rank = carry
        within = col - k * slots
        live = (within >= 0) & (within < counts[k])
        return first + counts[k], jnp.where(live, first + within, rank)

    return lax.fori_loop(0, shards, step, (jnp.int32(0), jnp.full((8, width), -1, jnp.int32)))[1]


def labels(counts, slots, width):
    shards = counts.shape[0]
    col = lax.broadcasted_iota(jnp.int32, (8, width), 1)

    def step(k, carry):
        last, label = carry
        last = last + counts[k]
        return last, label + jnp.where(col >= last, slots - counts[k], 0)

    return lax.fori_loop(0, shards, step, (jnp.int32(0), col))[1]


def compute_kernel(
    slots, live, dcnt, acnt, x_ref, comb_ref, w_ref, grad_ref, sums_ref,
    d_s, dt_s, a_s, cols_s, lab_s, out_s, sem,
):
    t = pl.program_id(0)
    tissues = pl.num_programs(0)
    sites, width = x_ref.shape[0], x_ref.shape[1] // 2
    rows, padded = d_s.shape[0], a_s.shape[0]
    parts, _, chunk = dt_s.shape
    depth = out_s.shape[1]
    scale = width ** (-0.5)

    @pl.when(t == 0)
    def _():
        rank_d = ranks(dcnt, slots, sites)[:1]
        rank_a = ranks(acnt, slots, sites)[:1]
        lab_s[...] = labels(acnt, slots, padded)
        comb = comb_ref[...]
        mask = (comb & 1).astype(F32)
        low = ((comb >> 1) & 255).astype(F32)
        high = (comb >> 9).astype(F32)
        table = jnp.concatenate([mask, low, high], axis=0).astype(BF16)
        for c in range(parts):
            row = lax.broadcasted_iota(jnp.int32, (chunk, sites), 0) + c * chunk
            pick = jnp.where(row == rank_d, 1.0, 0.0).astype(BF16)
            d = jnp.dot(pick, x_ref[:, :width], preferred_element_type=F32)
            d_s[c * chunk : (c + 1) * chunk, :] = d.astype(BF16)
            dt_s[c] = jnp.transpose(d).astype(BF16)
            cols_s[c * chunk : (c + 1) * chunk, :] = lax.dot_general(
                pick, table, (((1,), (1,)), ((), ())), preferred_element_type=F32
            )
        step = row_chunk(padded, 512)
        for c in range(padded // step):
            row = lax.broadcasted_iota(jnp.int32, (step, sites), 0) + c * step
            pick = jnp.where(row == rank_a, 1.0, 0.0).astype(BF16)
            a_s[c * step : (c + 1) * step, :] = jnp.dot(
                pick, x_ref[:, width:], preferred_element_type=F32
            ).astype(BF16)
        sums_ref[...] = jnp.zeros_like(sums_ref)

    lane = lax.broadcasted_iota(jnp.int32, (1, padded), 1)
    valid = lane < live
    label = lab_s[:1, :]
    tis = comb_ref.shape[0]
    pick_lane = lax.broadcasted_iota(jnp.int32, (chunk, 3 * tis), 1)
    don = lax.axis_index("don")
    start = pl.multiple_of(don * depth, depth)
    total = jnp.zeros((depth, padded), F32)
    lost = jnp.zeros((), F32)
    count = jnp.zeros((), F32)
    for c in range(parts):
        span = slice(c * chunk, (c + 1) * chunk)
        proj = jnp.dot(d_s[span, :], w_ref[0], preferred_element_type=F32).astype(BF16)
        score = (
            lax.dot_general(proj, a_s[...], (((1,), (1,)), ((), ())), preferred_element_type=F32)
            * scale
        )
        score = jnp.where(valid, score, -1e30)
        cols = cols_s[span, :]
        weight = jnp.sum(jnp.where(pick_lane == t, cols, 0.0), axis=1, keepdims=True)
        low = jnp.sum(jnp.where(pick_lane == t + tis, cols, 0.0), axis=1, keepdims=True)
        high = jnp.sum(jnp.where(pick_lane == t + 2 * tis, cols, 0.0), axis=1, keepdims=True)
        target = (high * 256.0 + low).astype(jnp.int32)
        highest = jnp.max(score, axis=1, keepdims=True)
        expo = jnp.where(valid, jnp.exp(score - highest), 0.0)
        summed = jnp.sum(expo, axis=1, keepdims=True)
        hit = label == target
        picked = jnp.sum(jnp.where(hit, score, 0.0), axis=1, keepdims=True)
        lost = lost + jnp.sum(weight * (highest + jnp.log(summed) - picked))
        count = count + jnp.sum(weight)
        prob = expo * (weight / summed)
        dscore = jnp.where(hit, prob - weight, prob).astype(BF16)
        total = total + jnp.dot(
            dt_s[c, pl.ds(start, depth), :], dscore, preferred_element_type=F32
        )
    total = total * scale
    slot = lax.rem(t, 2)

    def out_copy(which, at):
        return pltpu.make_async_copy(out_s.at[which], grad_ref.at[:, at, :], sem.at[which])

    @pl.when(t >= 2)
    def _():
        out_copy(slot, t - 2).wait()

    out_s[slot] = jnp.dot(total.astype(BF16), a_s[...], preferred_element_type=F32)
    out_copy(slot, t).start()
    first = lax.broadcasted_iota(jnp.int32, sums_ref.shape, 0) == 0
    sums_ref[...] += jnp.where(first, lost, count)

    @pl.when(t == tissues - 1)
    def _():
        out_copy(1 - slot, t - 1).wait()
        out_copy(slot, t).wait()


def compute(slots, donors_all, dcnt, acnt, x, comb, weights, depth):
    tissues, width = weights.shape[0], weights.shape[1]
    sites = x.shape[0]
    shards = acnt.shape[0]
    live = shards * (slots + 1) // 2
    rows = round_up(live, 16)
    padded = round_up(live, 128)
    chunk = row_chunk(rows)
    return pl.pallas_call(
        functools.partial(compute_kernel, slots, live),
        grid=(tissues,),
        in_specs=[
            pl.BlockSpec(memory_space=pltpu.SMEM),
            pl.BlockSpec(memory_space=pltpu.SMEM),
            pl.BlockSpec(memory_space=pltpu.VMEM),
            pl.BlockSpec(memory_space=pltpu.VMEM),
            pl.BlockSpec((1, width, width), lambda t: (t, 0, 0)),
        ],
        out_specs=[
            pl.BlockSpec(memory_space=pl.ANY),
            pl.BlockSpec((8, 128), lambda t: (0, 0)),
        ],
        out_shape=[
            jax.ShapeDtypeStruct((depth, tissues, width), F32),
            jax.ShapeDtypeStruct((8, 128), F32),
        ],
        scratch_shapes=[
            pltpu.VMEM((rows, width), BF16),
            pltpu.VMEM((rows // chunk, width, chunk), BF16),
            pltpu.VMEM((padded, width), BF16),
            pltpu.VMEM((rows, 3 * tissues), F32),
            pltpu.VMEM((8, padded), jnp.int32),
            pltpu.VMEM((2, depth, width), F32),
            pltpu.SemaphoreType.DMA((2,)),
        ],
        compiler_params=pltpu.CompilerParams(vmem_limit_bytes=60 * 1024 * 1024),
    )(dcnt, acnt, x, comb, weights)


def local(
    don_size,
    donor_emb,
    acceptor_emb,
    donor_pos,
    acceptor_pos,
    donor_count,
    acceptor_count,
    target,
    junction_mask,
    weights,
):
    slots = donor_pos.shape[0]
    tis_dev, width = weights.shape[0], weights.shape[1]
    column = lax.axis_index("acc")
    donor_local = donor_emb.at[donor_pos].get(mode="promise_in_bounds")
    acceptor_local = acceptor_emb.at[acceptor_pos].get(mode="promise_in_bounds")
    mine = jnp.concatenate([donor_local, acceptor_local], axis=1)
    x = lax.all_gather(mine, ("don", "acc"), axis=0, tiled=True)
    dcnt = lax.all_gather(donor_count, "don", axis=0, tiled=True)
    comb = lax.dynamic_slice_in_dim(target * 2 + junction_mask, column * tis_dev, tis_dev, 0)
    comb = lax.all_gather(comb, "don", axis=1, tiled=True)
    grad_weight, sums = compute(
        slots, None, dcnt, acceptor_count, x, comb, weights, width // don_size
    )
    sums = lax.psum(sums[:2, 0], "acc")
    return sums[0] / jnp.maximum(sums[1], 1.0), grad_weight


def solution(mesh):
    return jax.shard_map(
        functools.partial(local, mesh.shape["don"]),
        mesh=mesh,
        in_specs=(
            P(("don", "acc"), None),
            P(("don", "acc"), None),
            P(("don", "acc")),
            P(("don", "acc")),
            P("don"),
            P(),
            P(None, "don"),
            P(None, "don"),
            P("acc", None, None),
        ),
        out_specs=(P(), P("don", "acc", None)),
        check_vma=False,
    )
```

```python
import functools

import jax
import jax.numpy as jnp
from jax import lax
from jax.experimental import pallas as pl
from jax.experimental.pallas import tpu as pltpu
from jax.sharding import PartitionSpec as P

BF16 = jnp.bfloat16
F32 = jnp.float32


def round_up(n, m):
    return (n + m - 1) // m * m


def row_chunk(n, limit=416):
    best = 16
    for r in range(16, limit + 1, 16):
        if n % r == 0:
            best = r
    return best


def ranks(counts, slots, width):
    shards = counts.shape[0]
    col = lax.broadcasted_iota(jnp.int32, (8, width), 1)

    def step(k, carry):
        first, rank = carry
        within = col - k * slots
        live = (within >= 0) & (within < counts[k])
        return first + counts[k], jnp.where(live, first + within, rank)

    return lax.fori_loop(0, shards, step, (jnp.int32(0), jnp.full((8, width), -1, jnp.int32)))[1]


def labels(counts, slots, width):
    shards = counts.shape[0]
    col = lax.broadcasted_iota(jnp.int32, (8, width), 1)

    def step(k, carry):
        last, label = carry
        last = last + counts[k]
        return last, label + jnp.where(col >= last, slots - counts[k], 0)

    return lax.fori_loop(0, shards, step, (jnp.int32(0), col))[1]


def compute_kernel(
    slots, live, dcnt, acnt, x_ref, comb_ref, w_ref, grad_ref, sums_ref,
    d_s, dt_s, a_s, cols_s, lab_s, out_s, sem,
):
    t = pl.program_id(0)
    tissues = pl.num_programs(0)
    sites, width = x_ref.shape[0], x_ref.shape[1] // 2
    rows, padded = d_s.shape[0], a_s.shape[0]
    parts, _, chunk = dt_s.shape
    depth = out_s.shape[1]
    scale = width ** (-0.5)

    @pl.when(t == 0)
    def _():
        rank_d = ranks(dcnt, slots, sites)[:1]
        rank_a = ranks(acnt, slots, sites)[:1]
        lab_s[...] = labels(acnt, slots, padded)
        comb = comb_ref[...]
        mask = (comb & 1).astype(F32)
        low = ((comb >> 1) & 255).astype(F32)
        high = (comb >> 9).astype(F32)
        table = jnp.concatenate([mask, low, high], axis=0).astype(BF16)
        for c in range(parts):
            row = lax.broadcasted_iota(jnp.int32, (chunk, sites), 0) + c * chunk
            pick = jnp.where(row == rank_d, 1.0, 0.0).astype(BF16)
            d = jnp.dot(pick, x_ref[:, :width], preferred_element_type=F32)
            d_s[c * chunk : (c + 1) * chunk, :] = d.astype(BF16)
            dt_s[c] = jnp.transpose(d).astype(BF16)
            cols_s[c * chunk : (c + 1) * chunk, :] = lax.dot_general(
                pick, table, (((1,), (1,)), ((), ())), preferred_element_type=F32
            )
        step = row_chunk(padded, 512)
        for c in range(padded // step):
            row = lax.broadcasted_iota(jnp.int32, (step, sites), 0) + c * step
            pick = jnp.where(row == rank_a, 1.0, 0.0).astype(BF16)
            a_s[c * step : (c + 1) * step, :] = jnp.dot(
                pick, x_ref[:, width:], preferred_element_type=F32
            ).astype(BF16)
        sums_ref[...] = jnp.zeros_like(sums_ref)

    lane = lax.broadcasted_iota(jnp.int32, (1, padded), 1)
    valid = lane < live
    label = lab_s[:1, :]
    tis = comb_ref.shape[0]
    pick_lane = lax.broadcasted_iota(jnp.int32, (chunk, 3 * tis), 1)
    don = lax.axis_index("don")
    start = pl.multiple_of(don * depth, depth)
    total = jnp.zeros((depth, padded), F32)
    lost = jnp.zeros((), F32)
    count = jnp.zeros((), F32)
    for c in range(parts):
        span = slice(c * chunk, (c + 1) * chunk)
        proj = jnp.dot(d_s[span, :], w_ref[0], preferred_element_type=F32).astype(BF16)
        score = (
            lax.dot_general(proj, a_s[...], (((1,), (1,)), ((), ())), preferred_element_type=F32)
            * scale
        )
        score = jnp.where(valid, score, -1e30)
        cols = cols_s[span, :]
        weight = jnp.sum(jnp.where(pick_lane == t, cols, 0.0), axis=1, keepdims=True)
        low = jnp.sum(jnp.where(pick_lane == t + tis, cols, 0.0), axis=1, keepdims=True)
        high = jnp.sum(jnp.where(pick_lane == t + 2 * tis, cols, 0.0), axis=1, keepdims=True)
        target = (high * 256.0 + low).astype(jnp.int32)
        highest = jnp.max(score, axis=1, keepdims=True)
        expo = jnp.where(valid, jnp.exp(score - highest), 0.0)
        summed = jnp.sum(expo, axis=1, keepdims=True)
        hit = label == target
        picked = jnp.sum(jnp.where(hit, score, 0.0), axis=1, keepdims=True)
        lost = lost + jnp.sum(weight * (highest + jnp.log(summed) - picked))
        count = count + jnp.sum(weight)
        prob = expo * (weight / summed)
        dscore = jnp.where(hit, prob - weight, prob).astype(BF16)
        total = total + jnp.dot(
            dt_s[c, pl.ds(start, depth), :], dscore, preferred_element_type=F32
        )
    total = total * scale
    slot = lax.rem(t, 2)

    def out_copy(which, at):
        return pltpu.make_async_copy(out_s.at[which], grad_ref.at[:, at, :], sem.at[which])

    @pl.when(t >= 2)
    def _():
        out_copy(slot, t - 2).wait()

    out_s[slot] = jnp.dot(total.astype(BF16), a_s[...], preferred_element_type=F32)
    out_copy(slot, t).start()
    first = lax.broadcasted_iota(jnp.int32, sums_ref.shape, 0) == 0
    sums_ref[...] += jnp.where(first, lost, count)

    @pl.when(t == tissues - 1)
    def _():
        out_copy(1 - slot, t - 1).wait()
        out_copy(slot, t).wait()


def compute(slots, dcnt, acnt, x, comb, weights, depth):
    tissues, width = weights.shape[0], weights.shape[1]
    sites = x.shape[0]
    shards = acnt.shape[0]
    live = shards * (slots + 1) // 2
    rows = round_up(live, 16)
    padded = round_up(live, 128)
    chunk = row_chunk(rows)
    return pl.pallas_call(
        functools.partial(compute_kernel, slots, live),
        grid=(tissues,),
        in_specs=[
            pl.BlockSpec(memory_space=pltpu.SMEM),
            pl.BlockSpec(memory_space=pltpu.SMEM),
            pl.BlockSpec(memory_space=pltpu.VMEM),
            pl.BlockSpec(memory_space=pltpu.VMEM),
            pl.BlockSpec((1, width, width), lambda t: (t, 0, 0)),
        ],
        out_specs=[
            pl.BlockSpec(memory_space=pl.ANY),
            pl.BlockSpec((8, 128), lambda t: (0, 0)),
        ],
        out_shape=[
            jax.ShapeDtypeStruct((depth, tissues, width), F32),
            jax.ShapeDtypeStruct((8, 128), F32),
        ],
        scratch_shapes=[
            pltpu.VMEM((rows, width), BF16),
            pltpu.VMEM((rows // chunk, width, chunk), BF16),
            pltpu.VMEM((padded, width), BF16),
            pltpu.VMEM((rows, 3 * tissues), F32),
            pltpu.VMEM((8, padded), jnp.int32),
            pltpu.VMEM((2, depth, width), F32),
            pltpu.SemaphoreType.DMA((2,)),
        ],
        compiler_params=pltpu.CompilerParams(vmem_limit_bytes=60 * 1024 * 1024),
    )(dcnt, acnt, x, comb, weights)


MESH = pl.DeviceIdType.MESH


def gather_kernel(don_size, acc_size, inner, x_ref, comb_ref, cnt_ref, xs_ref, combs_ref, cnts_ref,
                  send_sem, recv_sem, side_send, side_recv, own_sem):
    outer = acc_size // inner
    chips = don_size // 2
    alternate = chips == inner
    don, acc = lax.axis_index("don"), lax.axis_index("acc")
    core, x = lax.rem(don, 2), don // 2
    o, i = acc // inner, lax.rem(acc, inner)
    if alternate:
        b = core * x + (1 - core) * i
        c = core * i + (1 - core) * x
        b_size, c_size = inner, inner
    else:
        b, c, b_size, c_size = i, x, inner, chips

    def place(which, oo, bb, cc):
        if alternate:
            xx = core * bb + (1 - core) * cc
            ii = core * cc + (1 - core) * bb
        else:
            xx, ii = cc, bb
        return (xx * 2 + which, oo * inner + ii)

    def away(at, k, size):
        return lax.rem(at + k, size)

    peers = [place(core, away(o, k, outer), b, c) for k in range(1, outer)]
    peers += [place(core, o, away(b, k, b_size), c) for k in range(1, b_size)]
    peers += [place(core, o, b, away(c, k, c_size)) for k in range(1, c_size)]
    peers += [place(1 - core, o, b, c)]
    others = [(lax.rem(don + k, don_size), acc) for k in range(1, don_size)]
    barrier = pltpu.get_barrier_semaphore()
    for peer in peers + others:
        pl.semaphore_signal(barrier, inc=1, device_id=peer, device_id_type=MESH)
    pl.semaphore_wait(barrier, len(peers) + len(others))

    sent = []
    held = don * acc_size + acc

    def send(source, slot, peer):
        copy = pltpu.make_async_remote_copy(
            src_ref=source,
            dst_ref=xs_ref.at[slot],
            send_sem=send_sem.at[len(sent)],
            recv_sem=recv_sem.at[slot],
            device_id=peer,
            device_id_type=MESH,
        )
        copy.start()
        sent.append(copy)

    def slot_of(at):
        return at[0] * acc_size + at[1]

    def arrived(slot):
        pltpu.make_async_copy(x_ref, xs_ref.at[slot], recv_sem.at[slot]).wait()

    def forward(source, slot, hops):
        if hops >= 3:
            for k in range(1, outer):
                send(source, slot, place(core, away(o, k, outer), b, c))
        if hops >= 2:
            for k in range(1, b_size):
                send(source, slot, place(core, o, away(b, k, b_size), c))
        if hops >= 1:
            for k in range(1, c_size):
                send(source, slot, place(core, o, b, away(c, k, c_size)))
        send(source, slot, place(1 - core, o, b, c))

    forward(x_ref, held, 3)
    side = []
    for k, peer in enumerate(others):
        for j, (source, target) in enumerate(((comb_ref, combs_ref), (cnt_ref, cnts_ref))):
            copy = pltpu.make_async_remote_copy(
                src_ref=source,
                dst_ref=target.at[don],
                send_sem=side_send.at[k, j],
                recv_sem=side_recv.at[k, j],
                device_id=peer,
                device_id_type=MESH,
            )
            copy.start()
            side.append(copy)
    own = [
        pltpu.make_async_copy(x_ref, xs_ref.at[held], own_sem.at[0]),
        pltpu.make_async_copy(comb_ref, combs_ref.at[don], own_sem.at[1]),
        pltpu.make_async_copy(cnt_ref, cnts_ref.at[don], own_sem.at[2]),
    ]
    for copy in own:
        copy.start()

    def relay(slot, hops):
        arrived(slot)
        forward(xs_ref.at[slot], slot, hops)

    for ko in range(outer):
        oo = away(o, ko, outer)
        if ko:
            relay(slot_of(place(core, oo, b, c)), 2)
        for kb in range(1, b_size):
            relay(slot_of(place(core, oo, away(b, kb, b_size), c)), 1)
    for ko in range(outer):
        for kb in range(b_size):
            for kc in range(1, c_size):
                relay(slot_of(place(core, away(o, ko, outer), away(b, kb, b_size), away(c, kc, c_size))), 0)
    for ko in range(outer):
        for kx in range(chips):
            for ki in range(inner):
                at = (away(x, kx, chips) * 2 + 1 - core, away(o, ko, outer) * inner + away(i, ki, inner))
                arrived(slot_of(at))
    for copy in sent:
        copy.wait_send()
    for copy in side:
        copy.wait()
    for copy in own:
        copy.wait()


def gather(don_size, acc_size, x, comb, counts):
    inner = 1
    while (2 * inner) ** 2 <= acc_size:
        inner *= 2
    outer, chips = acc_size // inner, don_size // 2
    half = don_size * acc_size // 2
    per_core = (outer - 1) + outer * (inner - 1) + outer * inner * (chips - 1)
    any_space = pl.BlockSpec(memory_space=pl.ANY)
    shards = don_size * acc_size
    return pl.pallas_call(
        functools.partial(gather_kernel, don_size, acc_size, inner),
        in_specs=[any_space] * 3,
        out_specs=[any_space] * 3,
        out_shape=[
            jax.ShapeDtypeStruct((shards,) + x.shape, x.dtype),
            jax.ShapeDtypeStruct((don_size,) + comb.shape, comb.dtype),
            jax.ShapeDtypeStruct((don_size,) + counts.shape, counts.dtype),
        ],
        scratch_shapes=[
            pltpu.SemaphoreType.DMA((per_core + half,)),
            pltpu.SemaphoreType.DMA((shards,)),
            pltpu.SemaphoreType.DMA((don_size - 1, 2)),
            pltpu.SemaphoreType.DMA((don_size - 1, 2)),
            pltpu.SemaphoreType.DMA((3,)),
        ],
        compiler_params=pltpu.CompilerParams(collective_id=0, has_side_effects=True),
    )(x, comb, counts)


def loss_kernel(acc_size, sums_ref, loss_ref, land, send_sem, recv_sem, own_sem):
    don, acc = lax.axis_index("don"), lax.axis_index("acc")
    peers = [(don, lax.rem(acc + k, acc_size)) for k in range(1, acc_size)]
    barrier = pltpu.get_barrier_semaphore()
    for peer in peers:
        pl.semaphore_signal(barrier, inc=1, device_id=peer, device_id_type=MESH)
    pl.semaphore_wait(barrier, acc_size - 1)
    copies = []
    for k, peer in enumerate(peers):
        copy = pltpu.make_async_remote_copy(
            src_ref=sums_ref,
            dst_ref=land.at[acc],
            send_sem=send_sem.at[k],
            recv_sem=recv_sem.at[k],
            device_id=peer,
            device_id_type=MESH,
        )
        copy.start()
        copies.append(copy)
    own = pltpu.make_async_copy(sums_ref, land.at[acc], own_sem)
    own.start()
    own.wait()
    for copy in copies:
        copy.wait()
    total = land[0]
    for k in range(1, acc_size):
        total = total + land[k]
    loss_ref[...] = jnp.broadcast_to(total[:1] / jnp.maximum(total[1:2], 1.0), loss_ref.shape)


def loss_sum(acc_size, sums):
    return pl.pallas_call(
        functools.partial(loss_kernel, acc_size),
        in_specs=[pl.BlockSpec(memory_space=pltpu.VMEM)],
        out_specs=pl.BlockSpec(memory_space=pltpu.VMEM),
        out_shape=jax.ShapeDtypeStruct(sums.shape, F32),
        scratch_shapes=[
            pltpu.VMEM((acc_size,) + sums.shape, F32),
            pltpu.SemaphoreType.DMA((acc_size - 1,)),
            pltpu.SemaphoreType.DMA((acc_size - 1,)),
            pltpu.SemaphoreType.DMA,
        ],
        compiler_params=pltpu.CompilerParams(collective_id=1, has_side_effects=True),
    )(sums)


def local(
    don_size,
    acc_size,
    donor_emb,
    acceptor_emb,
    donor_pos,
    acceptor_pos,
    donor_count,
    acceptor_count,
    target,
    junction_mask,
    weights,
):
    slots = donor_pos.shape[0]
    tis_dev, width = weights.shape[0], weights.shape[1]
    column = lax.axis_index("acc")
    donor_local = donor_emb.at[donor_pos].get(mode="promise_in_bounds")
    acceptor_local = acceptor_emb.at[acceptor_pos].get(mode="promise_in_bounds")
    mine = jnp.concatenate([donor_local, acceptor_local], axis=1)
    comb = lax.dynamic_slice_in_dim(target * 2 + junction_mask, column * tis_dev, tis_dev, 0)
    x, comb, dcnt = gather(don_size, acc_size, mine, comb, donor_count[None, :])
    x = x.reshape(-1, 2 * width)
    comb = jnp.transpose(comb, (1, 0, 2)).reshape(tis_dev, -1)
    grad_weight, sums = compute(
        slots, dcnt.reshape(-1), acceptor_count, x, comb, weights, width // don_size
    )
    return loss_sum(acc_size, sums)[0, 0], grad_weight


def solution(mesh):
    return jax.shard_map(
        functools.partial(local, mesh.shape["don"], mesh.shape["acc"]),
        mesh=mesh,
        in_specs=(
            P(("don", "acc"), None),
            P(("don", "acc"), None),
            P(("don", "acc")),
            P(("don", "acc")),
            P("don"),
            P(),
            P(None, "don"),
            P(None, "don"),
            P("acc", None, None),
        ),
        out_specs=(P(), P("don", "acc", None)),
        check_vma=False,
    )
```

```python
import functools

import jax
import jax.numpy as jnp
from jax import lax
from jax.experimental import pallas as pl
from jax.experimental.pallas import tpu as pltpu
from jax.sharding import PartitionSpec as P

BF16 = jnp.bfloat16
F32 = jnp.float32


def round_up(n, m):
    return (n + m - 1) // m * m


def row_chunk(n, limit=416):
    best = 16
    for r in range(16, limit + 1, 16):
        if n % r == 0:
            best = r
    return best


def ranks(counts, slots, width):
    groups, _, each = counts.shape
    shards = groups * each
    col = lax.broadcasted_iota(jnp.int32, (8, width), 1)

    def step(k, carry):
        first, rank = carry
        number = counts[k // each, 0, lax.rem(k, each)]
        within = col - k * slots
        live = (within >= 0) & (within < number)
        return first + number, jnp.where(live, first + within, rank)

    return lax.fori_loop(0, shards, step, (jnp.int32(0), jnp.full((8, width), -1, jnp.int32)))[1]


def labels(counts, slots, width):
    shards = counts.shape[2]
    col = lax.broadcasted_iota(jnp.int32, (8, width), 1)

    def step(k, carry):
        last, label = carry
        last = last + counts[0, 0, k]
        return last, label + jnp.where(col >= last, slots - counts[0, 0, k], 0)

    return lax.fori_loop(0, shards, step, (jnp.int32(0), col))[1]


def compute_kernel(
    slots, live, dcnt, acnt, x_ref, comb_ref, w_ref, grad_ref, sums_ref,
    d_s, dt_s, a_s, cols_s, lab_s, lost_s, out_s, sem,
):
    t = pl.program_id(0)
    tissues = pl.num_programs(0)
    sites, width = x_ref.shape[0], x_ref.shape[1] // 2
    rows, padded = d_s.shape[0], a_s.shape[0]
    parts, _, chunk = dt_s.shape
    depth = out_s.shape[1]
    scale = width ** (-0.5)

    @pl.when(t == 0)
    def _():
        rank_d = ranks(dcnt, slots, sites)[:1]
        rank_a = ranks(acnt, slots, sites)[:1]
        lab_s[...] = labels(acnt, slots, padded)
        comb = jnp.concatenate([comb_ref[p] for p in range(comb_ref.shape[0])], axis=1)
        mask = (comb & 1).astype(F32)
        low = ((comb >> 1) & 255).astype(F32)
        high = (comb >> 9).astype(F32)
        table = jnp.concatenate([mask, low], axis=0).astype(BF16)
        upper = jnp.concatenate([jnp.zeros_like(high), high], axis=0).astype(BF16)
        for c in range(parts):
            row = lax.broadcasted_iota(jnp.int32, (chunk, sites), 0) + c * chunk
            pick = jnp.where(row == rank_d, 1.0, 0.0).astype(BF16)
            d = jnp.dot(pick, x_ref[:, :width], preferred_element_type=F32)
            d_s[c * chunk : (c + 1) * chunk, :] = d.astype(BF16)
            dt_s[c] = jnp.transpose(d).astype(BF16)
            low_cols, high_cols = [
                lax.dot_general(pick, part, (((1,), (1,)), ((), ())), preferred_element_type=F32)
                for part in (table, upper)
            ]
            cols_s[c * chunk : (c + 1) * chunk, :] = low_cols + 256.0 * high_cols
        step = row_chunk(padded, 512)
        for c in range(padded // step):
            row = lax.broadcasted_iota(jnp.int32, (step, sites), 0) + c * step
            pick = jnp.where(row == rank_a, 1.0, 0.0).astype(BF16)
            a_s[c * step : (c + 1) * step, :] = jnp.dot(
                pick, x_ref[:, width:], preferred_element_type=F32
            ).astype(BF16)
        lost_s[...] = jnp.zeros_like(lost_s)

    lane = lax.broadcasted_iota(jnp.int32, (1, padded), 1)
    valid = lane < live
    label = lab_s[:1, :]
    tis = comb_ref.shape[1]
    pick_lane = lax.broadcasted_iota(jnp.int32, (chunk, 2 * tis), 1)
    don = lax.axis_index("don")
    start = pl.multiple_of(don * depth, depth)
    total = jnp.zeros((depth, padded), F32)
    for c in range(parts):
        span = slice(c * chunk, (c + 1) * chunk)
        proj = jnp.dot(d_s[span, :], w_ref[0], preferred_element_type=F32).astype(BF16)
        score = (
            lax.dot_general(proj, a_s[...], (((1,), (1,)), ((), ())), preferred_element_type=F32)
            * scale
        )
        score = jnp.where(valid, score, -1e30)
        cols = cols_s[span, :]
        weight = jnp.sum(jnp.where(pick_lane == t, cols, 0.0), axis=1, keepdims=True)
        target = jnp.sum(jnp.where(pick_lane == t + tis, cols, 0.0), axis=1, keepdims=True)
        target = target.astype(jnp.int32)
        highest = jnp.max(score, axis=1, keepdims=True)
        expo = jnp.where(valid, jnp.exp(score - highest), 0.0)
        summed = jnp.sum(expo, axis=1, keepdims=True)
        hit = label == target
        picked = jnp.sum(jnp.where(hit, score, 0.0), axis=1, keepdims=True)
        lost_s[0] += weight * (highest + jnp.log(summed) - picked)
        lost_s[1] += weight
        prob = expo * (weight / summed)
        dscore = jnp.where(hit, prob - weight, prob).astype(BF16)
        total = total + jnp.dot(
            dt_s[c, pl.ds(start, depth), :], dscore, preferred_element_type=F32
        )
    total = total * scale
    slot = lax.rem(t, 2)

    def out_copy(which, at):
        return pltpu.make_async_copy(out_s.at[which], grad_ref.at[:, at, :], sem.at[which])

    @pl.when(t >= 2)
    def _():
        out_copy(slot, t - 2).wait()

    out_s[slot] = jnp.dot(total.astype(BF16), a_s[...], preferred_element_type=F32)
    out_copy(slot, t).start()

    @pl.when(t == tissues - 1)
    def _():
        first = lax.broadcasted_iota(jnp.int32, sums_ref.shape, 0) == 0
        sums_ref[...] = jnp.where(first, jnp.sum(lost_s[0]), jnp.sum(lost_s[1]))
        out_copy(1 - slot, t - 1).wait()
        out_copy(slot, t).wait()


def compute(slots, dcnt, acnt, x, comb, weights, depth):
    tissues, width = weights.shape[0], weights.shape[1]
    sites = x.shape[0]
    shards = acnt.shape[2]
    live = shards * (slots + 1) // 2
    rows = round_up(live, 16)
    padded = round_up(live, 128)
    chunk = row_chunk(rows)
    return pl.pallas_call(
        functools.partial(compute_kernel, slots, live),
        grid=(tissues,),
        in_specs=[
            pl.BlockSpec(memory_space=pltpu.SMEM),
            pl.BlockSpec(memory_space=pltpu.SMEM),
            pl.BlockSpec(memory_space=pltpu.VMEM),
            pl.BlockSpec(memory_space=pltpu.VMEM),
            pl.BlockSpec((1, width, width), lambda t: (t, 0, 0)),
        ],
        out_specs=[
            pl.BlockSpec(memory_space=pl.ANY),
            pl.BlockSpec((8, 128), lambda t: (0, 0)),
        ],
        out_shape=[
            jax.ShapeDtypeStruct((depth, tissues, width), F32),
            jax.ShapeDtypeStruct((8, 128), F32),
        ],
        scratch_shapes=[
            pltpu.VMEM((rows, width), BF16),
            pltpu.VMEM((rows // chunk, width, chunk), BF16),
            pltpu.VMEM((padded, width), BF16),
            pltpu.VMEM((rows, 2 * tissues), F32),
            pltpu.VMEM((8, padded), jnp.int32),
            pltpu.VMEM((2, chunk, 1), F32),
            pltpu.VMEM((2, depth, width), F32),
            pltpu.SemaphoreType.DMA((2,)),
        ],
        compiler_params=pltpu.CompilerParams(vmem_limit_bytes=60 * 1024 * 1024),
    )(dcnt, acnt, x, comb, weights)


GROUP = 16


def fetch_kernel(
    dpos, apos, demb_ref, aemb_ref, target_ref, mask_ref, x_ref, comb_ref, dbuf, abuf, sem
):
    slots, width = x_ref.shape[0], x_ref.shape[1] // 2
    sides = ((dpos, demb_ref, dbuf, 0), (apos, aemb_ref, abuf, 1))
    for pos, emb, buf, which in sides:
        for k in range(slots):
            first = pl.multiple_of(pos[k] // GROUP * GROUP, GROUP)
            pltpu.make_async_copy(
                emb.at[pl.ds(first, GROUP), :],
                buf.at[pl.ds(k * GROUP, GROUP), :],
                sem.at[which],
            ).start()
    tis = comb_ref.shape[0]
    acc = lax.axis_index("acc")
    comb = target_ref[...] * 2 + mask_ref[...]
    mine = comb[:tis]
    for k in range(1, comb.shape[0] // tis):
        mine = jnp.where(acc == k, comb[k * tis : (k + 1) * tis], mine)
    comb_ref[...] = mine
    row = lax.broadcasted_iota(jnp.int32, (slots, slots * GROUP), 0)
    lane = lax.broadcasted_iota(jnp.int32, (slots, slots * GROUP), 1)
    for pos, emb, buf, which in sides:
        want = jnp.zeros((slots, slots * GROUP), jnp.int32)
        for k in range(slots):
            want = jnp.where(row == k, k * GROUP + lax.rem(pos[k], GROUP), want)
        pick = jnp.where(lane == want, 1.0, 0.0).astype(BF16)
        pltpu.make_async_copy(emb.at[pl.ds(0, slots * GROUP), :], buf, sem.at[which]).wait()
        x_ref[:, which * width : (which + 1) * width] = jnp.dot(
            pick, buf[...], preferred_element_type=F32
        ).astype(BF16)


def fetch(dpos, apos, demb, aemb, target, mask, tissues):
    slots, width = dpos.shape[0], demb.shape[1]
    smem = pl.BlockSpec(memory_space=pltpu.SMEM)
    hbm = pl.BlockSpec(memory_space=pl.ANY)
    vmem = pl.BlockSpec(memory_space=pltpu.VMEM)
    return pl.pallas_call(
        fetch_kernel,
        in_specs=[smem, smem, hbm, hbm, vmem, vmem],
        out_specs=[vmem, vmem],
        out_shape=[
            jax.ShapeDtypeStruct((slots, 2 * width), BF16),
            jax.ShapeDtypeStruct((tissues, target.shape[1]), jnp.int32),
        ],
        scratch_shapes=[
            pltpu.VMEM((slots * GROUP, width), BF16),
            pltpu.VMEM((slots * GROUP, width), BF16),
            pltpu.SemaphoreType.DMA((2,)),
        ],
    )(dpos, apos, demb, aemb, target, mask)


MESH = pl.DeviceIdType.MESH


def gather_kernel(don_size, acc_size, inner, x_ref, comb_ref, cnt_ref, xs_ref, combs_ref, cnts_ref,
                  send_sem, recv_sem, side_send, side_recv, own_sem):
    outer = acc_size // inner
    chips = don_size // 2
    alternate = chips == inner
    don, acc = lax.axis_index("don"), lax.axis_index("acc")
    core, x = lax.rem(don, 2), don // 2
    o, i = acc // inner, lax.rem(acc, inner)
    if alternate:
        b = core * x + (1 - core) * i
        c = core * i + (1 - core) * x
        b_size, c_size = inner, inner
    else:
        b, c, b_size, c_size = i, x, inner, chips

    def place(which, oo, bb, cc):
        if alternate:
            xx = core * bb + (1 - core) * cc
            ii = core * cc + (1 - core) * bb
        else:
            xx, ii = cc, bb
        return (xx * 2 + which, oo * inner + ii)

    def away(at, k, size):
        return lax.rem(at + k, size)

    peers = [place(core, away(o, k, outer), b, c) for k in range(1, outer)]
    peers += [place(core, o, away(b, k, b_size), c) for k in range(1, b_size)]
    peers += [place(core, o, b, away(c, k, c_size)) for k in range(1, c_size)]
    peers += [place(1 - core, o, b, c)]
    others = [(lax.rem(don + k, don_size), acc) for k in range(1, don_size)]
    barrier = pltpu.get_barrier_semaphore()
    for peer in peers + others:
        pl.semaphore_signal(barrier, inc=1, device_id=peer, device_id_type=MESH)
    pl.semaphore_wait(barrier, len(peers) + len(others))

    sent = []
    held = don * acc_size + acc

    def send(source, slot, peer):
        copy = pltpu.make_async_remote_copy(
            src_ref=source,
            dst_ref=xs_ref.at[slot],
            send_sem=send_sem.at[len(sent)],
            recv_sem=recv_sem.at[slot],
            device_id=peer,
            device_id_type=MESH,
        )
        copy.start()
        sent.append(copy)

    def slot_of(at):
        return at[0] * acc_size + at[1]

    def arrived(slot):
        pltpu.make_async_copy(x_ref, xs_ref.at[slot], recv_sem.at[slot]).wait()

    def forward(source, slot, hops):
        if hops >= 3:
            for k in range(1, outer):
                send(source, slot, place(core, away(o, k, outer), b, c))
        if hops >= 2:
            for k in range(1, b_size):
                send(source, slot, place(core, o, away(b, k, b_size), c))
        if hops >= 1:
            for k in range(1, c_size):
                send(source, slot, place(core, o, b, away(c, k, c_size)))
        send(source, slot, place(1 - core, o, b, c))

    forward(x_ref, held, 3)
    side = []
    for k, peer in enumerate(others):
        for j, (source, target) in enumerate(((comb_ref, combs_ref), (cnt_ref, cnts_ref))):
            copy = pltpu.make_async_remote_copy(
                src_ref=source,
                dst_ref=target.at[don],
                send_sem=side_send.at[k, j],
                recv_sem=side_recv.at[k, j],
                device_id=peer,
                device_id_type=MESH,
            )
            copy.start()
            side.append(copy)
    own = [
        pltpu.make_async_copy(x_ref, xs_ref.at[held], own_sem.at[0]),
        pltpu.make_async_copy(comb_ref, combs_ref.at[don], own_sem.at[1]),
        pltpu.make_async_copy(cnt_ref, cnts_ref.at[don], own_sem.at[2]),
    ]
    for copy in own:
        copy.start()

    def relay(slot, hops):
        arrived(slot)
        forward(xs_ref.at[slot], slot, hops)

    for ko in range(outer):
        oo = away(o, ko, outer)
        if ko:
            relay(slot_of(place(core, oo, b, c)), 2)
        for kb in range(1, b_size):
            relay(slot_of(place(core, oo, away(b, kb, b_size), c)), 1)
    for ko in range(outer):
        for kb in range(b_size):
            for kc in range(1, c_size):
                relay(slot_of(place(core, away(o, ko, outer), away(b, kb, b_size), away(c, kc, c_size))), 0)
    for ko in range(outer):
        for kx in range(chips):
            for ki in range(inner):
                at = (away(x, kx, chips) * 2 + 1 - core, away(o, ko, outer) * inner + away(i, ki, inner))
                arrived(slot_of(at))
    for copy in sent:
        copy.wait_send()
    for copy in side:
        copy.wait()
    for copy in own:
        copy.wait()


def gather(don_size, acc_size, x, comb, counts):
    inner = 1
    while (2 * inner) ** 2 <= acc_size:
        inner *= 2
    outer, chips = acc_size // inner, don_size // 2
    half = don_size * acc_size // 2
    per_core = (outer - 1) + outer * (inner - 1) + outer * inner * (chips - 1)
    any_space = pl.BlockSpec(memory_space=pl.ANY)
    shards = don_size * acc_size
    return pl.pallas_call(
        functools.partial(gather_kernel, don_size, acc_size, inner),
        in_specs=[any_space] * 3,
        out_specs=[any_space] * 3,
        out_shape=[
            jax.ShapeDtypeStruct((shards,) + x.shape, x.dtype),
            jax.ShapeDtypeStruct((don_size,) + comb.shape, comb.dtype),
            jax.ShapeDtypeStruct((don_size,) + counts.shape, counts.dtype),
        ],
        scratch_shapes=[
            pltpu.SemaphoreType.DMA((per_core + half,)),
            pltpu.SemaphoreType.DMA((shards,)),
            pltpu.SemaphoreType.DMA((don_size - 1, 2)),
            pltpu.SemaphoreType.DMA((don_size - 1, 2)),
            pltpu.SemaphoreType.DMA((3,)),
        ],
        compiler_params=pltpu.CompilerParams(collective_id=0, has_side_effects=True),
    )(x, comb, counts)


def loss_kernel(acc_size, sums_ref, loss_ref, land, send_sem, recv_sem, own_sem):
    don, acc = lax.axis_index("don"), lax.axis_index("acc")
    peers = [(don, lax.rem(acc + k, acc_size)) for k in range(1, acc_size)]
    barrier = pltpu.get_barrier_semaphore()
    for peer in peers:
        pl.semaphore_signal(barrier, inc=1, device_id=peer, device_id_type=MESH)
    pl.semaphore_wait(barrier, acc_size - 1)
    copies = []
    for k, peer in enumerate(peers):
        copy = pltpu.make_async_remote_copy(
            src_ref=sums_ref,
            dst_ref=land.at[acc],
            send_sem=send_sem.at[k],
            recv_sem=recv_sem.at[k],
            device_id=peer,
            device_id_type=MESH,
        )
        copy.start()
        copies.append(copy)
    own = pltpu.make_async_copy(sums_ref, land.at[acc], own_sem)
    own.start()
    own.wait()
    for copy in copies:
        copy.wait()
    total = land[0]
    for k in range(1, acc_size):
        total = total + land[k]
    loss_ref[...] = jnp.broadcast_to(total[:1] / jnp.maximum(total[1:2], 1.0), loss_ref.shape)


def loss_sum(acc_size, sums):
    return pl.pallas_call(
        functools.partial(loss_kernel, acc_size),
        in_specs=[pl.BlockSpec(memory_space=pltpu.VMEM)],
        out_specs=pl.BlockSpec(memory_space=pltpu.VMEM),
        out_shape=jax.ShapeDtypeStruct(sums.shape, F32),
        scratch_shapes=[
            pltpu.VMEM((acc_size,) + sums.shape, F32),
            pltpu.SemaphoreType.DMA((acc_size - 1,)),
            pltpu.SemaphoreType.DMA((acc_size - 1,)),
            pltpu.SemaphoreType.DMA,
        ],
        compiler_params=pltpu.CompilerParams(collective_id=1, has_side_effects=True),
    )(sums)


def local(
    don_size,
    acc_size,
    donor_emb,
    acceptor_emb,
    donor_pos,
    acceptor_pos,
    donor_count,
    acceptor_count,
    target,
    junction_mask,
    weights,
):
    slots = donor_pos.shape[0]
    tis_dev, width = weights.shape[0], weights.shape[1]
    mine, comb = fetch(donor_pos, acceptor_pos, donor_emb, acceptor_emb, target, junction_mask, tis_dev)
    x, comb, dcnt = gather(don_size, acc_size, mine, comb, donor_count[None, :])
    x = x.reshape(-1, 2 * width)
    grad_weight, sums = compute(
        slots, dcnt, acceptor_count[None, None, :], x, comb, weights, width // don_size
    )
    return loss_sum(acc_size, sums)[0, 0], grad_weight


def solution(mesh):
    return jax.shard_map(
        functools.partial(local, mesh.shape["don"], mesh.shape["acc"]),
        mesh=mesh,
        in_specs=(
            P(("don", "acc"), None),
            P(("don", "acc"), None),
            P(("don", "acc")),
            P(("don", "acc")),
            P("don"),
            P(),
            P(None, "don"),
            P(None, "don"),
            P("acc", None, None),
        ),
        out_specs=(P(), P("don", "acc", None)),
        check_vma=False,
    )
```

```python
import functools

import jax
import jax.numpy as jnp
from jax import lax
from jax.experimental import pallas as pl
from jax.experimental.pallas import tpu as pltpu
from jax.sharding import PartitionSpec as P

BF16 = jnp.bfloat16
F32 = jnp.float32


def round_up(n, m):
    return (n + m - 1) // m * m


def row_chunk(n, limit=416):
    best = 16
    for r in range(16, limit + 1, 16):
        if n % r == 0:
            best = r
    return best


def ranks(counts, slots, width):
    groups, _, each = counts.shape
    shards = groups * each
    col = lax.broadcasted_iota(jnp.int32, (8, width), 1)

    def step(k, carry):
        first, rank = carry
        number = counts[k // each, 0, lax.rem(k, each)]
        within = col - k * slots
        live = (within >= 0) & (within < number)
        return first + number, jnp.where(live, first + within, rank)

    return lax.fori_loop(0, shards, step, (jnp.int32(0), jnp.full((8, width), -1, jnp.int32)))[1]


def labels(counts, slots, width):
    shards = counts.shape[2]
    col = lax.broadcasted_iota(jnp.int32, (8, width), 1)

    def step(k, carry):
        last, label = carry
        last = last + counts[0, 0, k]
        return last, label + jnp.where(col >= last, slots - counts[0, 0, k], 0)

    return lax.fori_loop(0, shards, step, (jnp.int32(0), col))[1]


def compute_kernel(
    slots, live, dcnt, acnt, x_ref, comb_ref, w_ref, grad_ref, sums_ref,
    d_s, dt_s, a_s, cols_s, lab_s, lost_s, out_s, sem,
):
    t = pl.program_id(0)
    tissues = pl.num_programs(0)
    sites, width = x_ref.shape[0], x_ref.shape[1] // 2
    rows, padded = d_s.shape[0], a_s.shape[0]
    parts, _, chunk = dt_s.shape
    depth = out_s.shape[1]
    scale = width ** (-0.5)

    @pl.when(t == 0)
    def _():
        rank_d = ranks(dcnt, slots, sites)[:1]
        rank_a = ranks(acnt, slots, sites)[:1]
        lab_s[...] = labels(acnt, slots, padded)
        comb = jnp.concatenate([comb_ref[p] for p in range(comb_ref.shape[0])], axis=1)
        mask = (comb & 1).astype(F32)
        low = ((comb >> 1) & 255).astype(F32)
        high = (comb >> 9).astype(F32)
        table = jnp.concatenate([mask, low], axis=0).astype(BF16)
        upper = jnp.concatenate([jnp.zeros_like(high), high], axis=0).astype(BF16)
        for c in range(parts):
            row = lax.broadcasted_iota(jnp.int32, (chunk, sites), 0) + c * chunk
            pick = jnp.where(row == rank_d, 1.0, 0.0).astype(BF16)
            d = jnp.dot(pick, x_ref[:, :width], preferred_element_type=F32)
            d_s[c * chunk : (c + 1) * chunk, :] = d.astype(BF16)
            dt_s[c] = jnp.transpose(d).astype(BF16)
            low_cols, high_cols = [
                lax.dot_general(pick, part, (((1,), (1,)), ((), ())), preferred_element_type=F32)
                for part in (table, upper)
            ]
            cols_s[c * chunk : (c + 1) * chunk, :] = low_cols + 256.0 * high_cols
        step = row_chunk(padded, 512)
        for c in range(padded // step):
            row = lax.broadcasted_iota(jnp.int32, (step, sites), 0) + c * step
            pick = jnp.where(row == rank_a, 1.0, 0.0).astype(BF16)
            a_s[c * step : (c + 1) * step, :] = jnp.dot(
                pick, x_ref[:, width:], preferred_element_type=F32
            ).astype(BF16)
        lost_s[...] = jnp.zeros_like(lost_s)

    lane = lax.broadcasted_iota(jnp.int32, (1, padded), 1)
    valid = lane < live
    label = lab_s[:1, :]
    tis = comb_ref.shape[1]
    pick_lane = lax.broadcasted_iota(jnp.int32, (chunk, 2 * tis), 1)
    don = lax.axis_index("don")
    start = pl.multiple_of(don * depth, depth)
    total = jnp.zeros((depth, padded), F32)
    for c in range(parts):
        span = slice(c * chunk, (c + 1) * chunk)
        proj = jnp.dot(d_s[span, :], w_ref[0], preferred_element_type=F32).astype(BF16)
        score = (
            lax.dot_general(proj, a_s[...], (((1,), (1,)), ((), ())), preferred_element_type=F32)
            * scale
        )
        score = jnp.where(valid, score, -1e30)
        cols = cols_s[span, :]
        weight = jnp.sum(jnp.where(pick_lane == t, cols, 0.0), axis=1, keepdims=True)
        target = jnp.sum(jnp.where(pick_lane == t + tis, cols, 0.0), axis=1, keepdims=True)
        target = target.astype(jnp.int32)
        highest = jnp.max(score, axis=1, keepdims=True)
        expo = jnp.where(valid, jnp.exp(score - highest), 0.0)
        summed = jnp.sum(expo, axis=1, keepdims=True)
        hit = label == target
        picked = jnp.sum(jnp.where(hit, score, 0.0), axis=1, keepdims=True)
        lost_s[0] += weight * (highest + jnp.log(summed) - picked)
        lost_s[1] += weight
        prob = expo * (weight / summed)
        dscore = jnp.where(hit, prob - weight, prob).astype(BF16)
        total = total + jnp.dot(
            dt_s[c, pl.ds(start, depth), :], dscore, preferred_element_type=F32
        )
    total = total * scale
    slot = lax.rem(t, 2)

    def out_copy(which, at):
        return pltpu.make_async_copy(out_s.at[which], grad_ref.at[:, at, :], sem.at[which])

    @pl.when(t >= 2)
    def _():
        out_copy(slot, t - 2).wait()

    out_s[slot] = jnp.dot(total.astype(BF16), a_s[...], preferred_element_type=F32)
    out_copy(slot, t).start()

    @pl.when(t == tissues - 1)
    def _():
        first = lax.broadcasted_iota(jnp.int32, sums_ref.shape, 0) == 0
        sums_ref[...] = jnp.where(first, jnp.sum(lost_s[0]), jnp.sum(lost_s[1]))
        out_copy(1 - slot, t - 1).wait()
        out_copy(slot, t).wait()


def compute(slots, dcnt, acnt, x, comb, weights, depth):
    tissues, width = weights.shape[0], weights.shape[1]
    sites = x.shape[0]
    shards = acnt.shape[2]
    live = shards * (slots + 1) // 2
    rows = round_up(live, 16)
    padded = round_up(live, 128)
    chunk = row_chunk(rows)
    return pl.pallas_call(
        functools.partial(compute_kernel, slots, live),
        grid=(tissues,),
        in_specs=[
            pl.BlockSpec(memory_space=pltpu.SMEM),
            pl.BlockSpec(memory_space=pltpu.SMEM),
            pl.BlockSpec(memory_space=pltpu.VMEM),
            pl.BlockSpec(memory_space=pltpu.VMEM),
            pl.BlockSpec((1, width, width), lambda t: (t, 0, 0)),
        ],
        out_specs=[
            pl.BlockSpec(memory_space=pl.ANY),
            pl.BlockSpec((8, 128), lambda t: (0, 0)),
        ],
        out_shape=[
            jax.ShapeDtypeStruct((depth, tissues, width), F32),
            jax.ShapeDtypeStruct((8, 128), F32),
        ],
        scratch_shapes=[
            pltpu.VMEM((rows, width), BF16),
            pltpu.VMEM((rows // chunk, width, chunk), BF16),
            pltpu.VMEM((padded, width), BF16),
            pltpu.VMEM((rows, 2 * tissues), F32),
            pltpu.VMEM((8, padded), jnp.int32),
            pltpu.VMEM((2, chunk, 1), F32),
            pltpu.VMEM((2, depth, width), F32),
            pltpu.SemaphoreType.DMA((2,)),
        ],
        compiler_params=pltpu.CompilerParams(vmem_limit_bytes=60 * 1024 * 1024),
    )(dcnt, acnt, x, comb, weights)


GROUP = 16


def fetch_kernel(
    dpos, apos, demb_ref, aemb_ref, target_ref, mask_ref, x_ref, comb_ref, dbuf, abuf, sem
):
    slots, width = x_ref.shape[0], x_ref.shape[1] // 2
    sides = ((dpos, demb_ref, dbuf, 0), (apos, aemb_ref, abuf, 1))
    for pos, emb, buf, which in sides:
        for k in range(slots):
            first = pl.multiple_of(pos[k] // GROUP * GROUP, GROUP)
            pltpu.make_async_copy(
                emb.at[pl.ds(first, GROUP), :],
                buf.at[pl.ds(k * GROUP, GROUP), :],
                sem.at[which],
            ).start()
    tis = comb_ref.shape[0]
    acc = lax.axis_index("acc")
    comb = target_ref[...] * 2 + mask_ref[...]
    mine = comb[:tis]
    for k in range(1, comb.shape[0] // tis):
        mine = jnp.where(acc == k, comb[k * tis : (k + 1) * tis], mine)
    comb_ref[...] = mine
    row = lax.broadcasted_iota(jnp.int32, (slots, slots * GROUP), 0)
    lane = lax.broadcasted_iota(jnp.int32, (slots, slots * GROUP), 1)
    for pos, emb, buf, which in sides:
        want = jnp.zeros((slots, slots * GROUP), jnp.int32)
        for k in range(slots):
            want = jnp.where(row == k, k * GROUP + lax.rem(pos[k], GROUP), want)
        pick = jnp.where(lane == want, 1.0, 0.0).astype(BF16)
        pltpu.make_async_copy(emb.at[pl.ds(0, slots * GROUP), :], buf, sem.at[which]).wait()
        x_ref[:, which * width : (which + 1) * width] = jnp.dot(
            pick, buf[...], preferred_element_type=F32
        ).astype(BF16)


def fetch(dpos, apos, demb, aemb, target, mask, tissues):
    slots, width = dpos.shape[0], demb.shape[1]
    smem = pl.BlockSpec(memory_space=pltpu.SMEM)
    hbm = pl.BlockSpec(memory_space=pl.ANY)
    vmem = pl.BlockSpec(memory_space=pltpu.VMEM)
    return pl.pallas_call(
        fetch_kernel,
        in_specs=[smem, smem, hbm, hbm, vmem, vmem],
        out_specs=[vmem, vmem],
        out_shape=[
            jax.ShapeDtypeStruct((slots, 2 * width), BF16),
            jax.ShapeDtypeStruct((tissues, target.shape[1]), jnp.int32),
        ],
        scratch_shapes=[
            pltpu.VMEM((slots * GROUP, width), BF16),
            pltpu.VMEM((slots * GROUP, width), BF16),
            pltpu.SemaphoreType.DMA((2,)),
        ],
    )(dpos, apos, demb, aemb, target, mask)


MESH = pl.DeviceIdType.MESH


def gather_kernel(don_size, acc_size, inner, x_ref, comb_ref, cnt_ref, xs_ref, combs_ref, cnts_ref,
                  send_sem, recv_sem, side_send, side_recv, own_sem):
    outer = acc_size // inner
    chips = don_size // 2
    alternate = chips == inner
    don, acc = lax.axis_index("don"), lax.axis_index("acc")
    core, x = lax.rem(don, 2), don // 2
    o, i = acc // inner, lax.rem(acc, inner)
    if alternate:
        b = core * x + (1 - core) * i
        c = core * i + (1 - core) * x
        b_size, c_size = inner, inner
    else:
        b, c, b_size, c_size = i, x, inner, chips

    def place(which, oo, bb, cc):
        if alternate:
            xx = core * bb + (1 - core) * cc
            ii = core * cc + (1 - core) * bb
        else:
            xx, ii = cc, bb
        return (xx * 2 + which, oo * inner + ii)

    def away(at, k, size):
        return lax.rem(at + k, size)

    peers = [place(core, away(o, k, outer), b, c) for k in range(1, outer)]
    peers += [place(core, o, away(b, k, b_size), c) for k in range(1, b_size)]
    peers += [place(core, o, b, away(c, k, c_size)) for k in range(1, c_size)]
    peers += [place(1 - core, o, b, c)]
    others = [(lax.rem(don + k, don_size), acc) for k in range(1, don_size)]
    barrier = pltpu.get_barrier_semaphore()
    for peer in peers + others:
        pl.semaphore_signal(barrier, inc=1, device_id=peer, device_id_type=MESH)
    pl.semaphore_wait(barrier, len(peers) + len(others))

    sent = []
    held = don * acc_size + acc

    def send(source, slot, peer):
        copy = pltpu.make_async_remote_copy(
            src_ref=source,
            dst_ref=xs_ref.at[slot],
            send_sem=send_sem.at[len(sent)],
            recv_sem=recv_sem.at[slot],
            device_id=peer,
            device_id_type=MESH,
        )
        copy.start()
        sent.append(copy)

    def slot_of(at):
        return at[0] * acc_size + at[1]

    def arrived(slot):
        pltpu.make_async_copy(x_ref, xs_ref.at[slot], recv_sem.at[slot]).wait()

    def forward(source, slot, hops):
        if hops >= 3:
            for k in range(1, outer):
                send(source, slot, place(core, away(o, k, outer), b, c))
        if hops >= 2:
            for k in range(1, b_size):
                send(source, slot, place(core, o, away(b, k, b_size), c))
        if hops >= 1:
            for k in range(1, c_size):
                send(source, slot, place(core, o, b, away(c, k, c_size)))
        send(source, slot, place(1 - core, o, b, c))

    forward(x_ref, held, 3)
    side = []
    for k, peer in enumerate(others):
        for j, (source, target) in enumerate(((comb_ref, combs_ref), (cnt_ref, cnts_ref))):
            copy = pltpu.make_async_remote_copy(
                src_ref=source,
                dst_ref=target.at[don],
                send_sem=side_send.at[k, j],
                recv_sem=side_recv.at[k, j],
                device_id=peer,
                device_id_type=MESH,
            )
            copy.start()
            side.append(copy)
    own = [
        pltpu.make_async_copy(x_ref, xs_ref.at[held], own_sem.at[0]),
        pltpu.make_async_copy(comb_ref, combs_ref.at[don], own_sem.at[1]),
        pltpu.make_async_copy(cnt_ref, cnts_ref.at[don], own_sem.at[2]),
    ]
    for copy in own:
        copy.start()

    def relay(slot, hops):
        arrived(slot)
        forward(xs_ref.at[slot], slot, hops)

    for ko in range(outer):
        oo = away(o, ko, outer)
        if ko:
            relay(slot_of(place(core, oo, b, c)), 2)
        for kb in range(1, b_size):
            relay(slot_of(place(core, oo, away(b, kb, b_size), c)), 1)
    for ko in range(outer):
        for kb in range(b_size):
            for kc in range(1, c_size):
                relay(slot_of(place(core, away(o, ko, outer), away(b, kb, b_size), away(c, kc, c_size))), 0)
    for ko in range(outer):
        for kx in range(chips):
            for ki in range(inner):
                at = (away(x, kx, chips) * 2 + 1 - core, away(o, ko, outer) * inner + away(i, ki, inner))
                arrived(slot_of(at))
    for copy in sent:
        copy.wait_send()
    for copy in side:
        copy.wait()
    for copy in own:
        copy.wait()


def gather(don_size, acc_size, x, comb, counts):
    inner = 1
    while (2 * inner) ** 2 <= acc_size:
        inner *= 2
    outer, chips = acc_size // inner, don_size // 2
    half = don_size * acc_size // 2
    per_core = (outer - 1) + outer * (inner - 1) + outer * inner * (chips - 1)
    any_space = pl.BlockSpec(memory_space=pl.ANY)
    shards = don_size * acc_size
    return pl.pallas_call(
        functools.partial(gather_kernel, don_size, acc_size, inner),
        in_specs=[pl.BlockSpec(memory_space=pltpu.VMEM), any_space, any_space],
        out_specs=[pl.BlockSpec(memory_space=pltpu.VMEM), any_space, any_space],
        out_shape=[
            jax.ShapeDtypeStruct((shards,) + x.shape, x.dtype),
            jax.ShapeDtypeStruct((don_size,) + comb.shape, comb.dtype),
            jax.ShapeDtypeStruct((don_size,) + counts.shape, counts.dtype),
        ],
        scratch_shapes=[
            pltpu.SemaphoreType.DMA((per_core + half,)),
            pltpu.SemaphoreType.DMA((shards,)),
            pltpu.SemaphoreType.DMA((don_size - 1, 2)),
            pltpu.SemaphoreType.DMA((don_size - 1, 2)),
            pltpu.SemaphoreType.DMA((3,)),
        ],
        compiler_params=pltpu.CompilerParams(collective_id=0, has_side_effects=True),
    )(x, comb, counts)


def loss_kernel(acc_size, sums_ref, loss_ref, land, send_sem, recv_sem, own_sem):
    don, acc = lax.axis_index("don"), lax.axis_index("acc")
    peers = [(don, lax.rem(acc + k, acc_size)) for k in range(1, acc_size)]
    barrier = pltpu.get_barrier_semaphore()
    for peer in peers:
        pl.semaphore_signal(barrier, inc=1, device_id=peer, device_id_type=MESH)
    pl.semaphore_wait(barrier, acc_size - 1)
    copies = []
    for k, peer in enumerate(peers):
        copy = pltpu.make_async_remote_copy(
            src_ref=sums_ref,
            dst_ref=land.at[acc],
            send_sem=send_sem.at[k],
            recv_sem=recv_sem.at[k],
            device_id=peer,
            device_id_type=MESH,
        )
        copy.start()
        copies.append(copy)
    own = pltpu.make_async_copy(sums_ref, land.at[acc], own_sem)
    own.start()
    own.wait()
    for copy in copies:
        copy.wait()
    total = land[0]
    for k in range(1, acc_size):
        total = total + land[k]
    loss_ref[...] = jnp.broadcast_to(total[:1] / jnp.maximum(total[1:2], 1.0), loss_ref.shape)


def loss_sum(acc_size, sums):
    return pl.pallas_call(
        functools.partial(loss_kernel, acc_size),
        in_specs=[pl.BlockSpec(memory_space=pltpu.VMEM)],
        out_specs=pl.BlockSpec(memory_space=pltpu.VMEM),
        out_shape=jax.ShapeDtypeStruct(sums.shape, F32),
        scratch_shapes=[
            pltpu.VMEM((acc_size,) + sums.shape, F32),
            pltpu.SemaphoreType.DMA((acc_size - 1,)),
            pltpu.SemaphoreType.DMA((acc_size - 1,)),
            pltpu.SemaphoreType.DMA,
        ],
        compiler_params=pltpu.CompilerParams(collective_id=1, has_side_effects=True),
    )(sums)


def local(
    don_size,
    acc_size,
    donor_emb,
    acceptor_emb,
    donor_pos,
    acceptor_pos,
    donor_count,
    acceptor_count,
    target,
    junction_mask,
    weights,
):
    slots = donor_pos.shape[0]
    tis_dev, width = weights.shape[0], weights.shape[1]
    mine, comb = fetch(donor_pos, acceptor_pos, donor_emb, acceptor_emb, target, junction_mask, tis_dev)
    x, comb, dcnt = gather(don_size, acc_size, mine, comb, donor_count[None, :])
    x = x.reshape(-1, 2 * width)
    grad_weight, sums = compute(
        slots, dcnt, acceptor_count[None, None, :], x, comb, weights, width // don_size
    )
    return loss_sum(acc_size, sums)[0, 0], grad_weight


def solution(mesh):
    return jax.shard_map(
        functools.partial(local, mesh.shape["don"], mesh.shape["acc"]),
        mesh=mesh,
        in_specs=(
            P(("don", "acc"), None),
            P(("don", "acc"), None),
            P(("don", "acc")),
            P(("don", "acc")),
            P("don"),
            P(),
            P(None, "don"),
            P(None, "don"),
            P("acc", None, None),
        ),
        out_specs=(P(), P("don", "acc", None)),
        check_vma=False,
    )
```
